32 devices in a mesh: grp: 2 (over x), tm: 16 (over z, y, core).
Axes of the slice: x: 2, y: 2, z: 4, core: 2. Of those that a mesh axis runs over, the one named last changes fastest.
Arguments:
- frames_in: bfloat16 [16384, 1536], P(('grp', 'tm')), parts along dimension 0, may hold values from -6 to 6
- frame_time: int32 [64], P('grp'), parts along dimension 0, may hold values from 0 to 31, each once
- norm_gain: float32 [1536], replicated, may hold values from 0.25 to 1.75
- w_query: bfloat16 [1536, 768], replicated, may hold values from -2 to 2
- w_key: bfloat16 [1536, 768], replicated, may hold values from -2 to 2
- w_value: bfloat16 [1536, 768], replicated, may hold values from -0.15625 to 0.15625
- w_output: bfloat16 [768, 1536], replicated, may hold values from -0.21875 to 0.21875
Outputs:
- attended: bfloat16 [16384, 1536], P(('grp', 'tm')), parts along dimension 0
The draws below stay inside these ranges and needn't reach their ends.
There are 2 independent parts, one for each index of `grp`. The reference program is written for one: setup_inputs(seed, part) draws one part's arguments, and reference() takes and returns one part's arrays. A program takes and returns all parts, laid end to end along the dimension named above; an argument that names none is the same for every part. Nothing has to cross between parts.
Inputs may be any that keep to these rules, and one draw needn't show every extreme that they name: `frame_time`: each of 0 to 31 stands once.
All inputs are finite; a program needn't handle non-finite values.
Results may differ from the reference program's by a relative error of at most 0.004.
The reference program's roundings to bfloat16 on the way count: a program that leaves them out, or rounds other values in their place, can miss the bound.
Values may be sent and summed in bfloat16 or wider, within the bound.
A program may use at most 128 MiB of HBM per device.

```python
import jax
import jax.numpy as jnp
from jax import lax

D = 1536
HEADS = 6
HD = 128
HH = 16
WW = 16
WIN = 8
POOL = 4
FRAMES = 32
PK = 16


def projection(key, salt):
    base = jnp.clip(jax.random.normal(jax.random.fold_in(key, salt), (D, HEADS * HD), jnp.float32), -6.0, 6.0) * D ** (-0.5)
    return jnp.clip(base, -2.0, 2.0)


def draw_w_query(key, part):
    return projection(key, 1).astype(jnp.bfloat16)


def draw_w_key(key, part):
    return projection(key, 2).astype(jnp.bfloat16)


def shard_levels(key, extent, split, smallest, top_value):
    def one(position, parts):
        steps = jax.random.uniform(jax.random.fold_in(jax.random.fold_in(key, 6), position), (parts,), jnp.float32, smallest / len(split), top_value / len(split))
        return jnp.repeat(jnp.exp(steps), extent[position] // parts).reshape((-1,) + (1,) * (len(extent) - position - 1))

    factor_of = one(*split[0])
    for cut in split[1:]:
        factor_of = factor_of * one(*cut)
    return factor_of


def normal_values(key, shape, deviation, reach, cuts=(), kind=jnp.bfloat16):
    result = jax.random.normal(key, shape, jnp.float32) * deviation
    if len(cuts) > 0:
        result = shard_levels(key, shape, cuts, -0.22, 0.18) * result
    return jnp.clip(result, min=-reach, max=reach).astype(kind)


def setup_inputs(seed: int = 0, part: int = 0) -> dict:
    key_of = jax.random.split(jax.random.key(seed), 8)
    part_keys = jax.random.split(jax.random.fold_in(key_of[7], part), 8)
    frames_in = normal_values(part_keys[0], (FRAMES * HH * WW, D), 1.0, 6.0, ((0, 16),))
    frame_time = jax.random.permutation(part_keys[1], FRAMES).astype(jnp.int32)
    norm_gain = jnp.clip(1.0 + 0.15 * jax.random.normal(key_of[2], (D,), jnp.float32), 0.25, 1.75)
    w_query = draw_w_query(jax.random.fold_in(key_of[7], 71), part)
    w_key = draw_w_key(jax.random.fold_in(key_of[7], 71), part)
    w_value = normal_values(key_of[5], (D, HEADS * HD), D ** -0.5, 0.15625)
    w_output = normal_values(key_of[6], (HEADS * HD, D), (HEADS * HD) ** -0.5, 0.21875)
    return {"frames_in": frames_in, "frame_time": frame_time, "norm_gain": norm_gain, "w_query": w_query, "w_key": w_key, "w_value": w_value, "w_output": w_output}


def normed_rows(frames_in, norm_gain):
    values_f = frames_in.astype(jnp.float32)
    scale = lax.rsqrt(lax.optimization_barrier(jnp.mean(values_f * values_f, axis=-1, keepdims=True)) + 1e-06)
    return (values_f * scale * norm_gain.astype(jnp.float32)).astype(jnp.bfloat16)

def to_windows(array, count):
    shaped = array.reshape(count, HH // WIN, WIN, WW // WIN, WIN, HEADS, HD)
    shaped = shaped.transpose(0, 1, 3, 2, 4, 5, 6)
    return shaped.reshape(count, HH // WIN * (WW // WIN), WIN * WIN, HEADS, HD)

def from_windows(array, count):
    shaped = array.reshape(count, HH // WIN, WW // WIN, WIN, WIN, HEADS * HD)
    shaped = shaped.transpose(0, 1, 3, 2, 4, 5)
    return shaped.reshape(count * HH * WW, HEADS * HD)

def pooled(array, count):
    shaped = array.reshape(count, HH // POOL, POOL, WW // POOL, POOL, HEADS * HD).astype(jnp.float32)
    return lax.optimization_barrier(jnp.mean(shaped, axis=(2, 4))).reshape(count * PK, HEADS, HD).astype(jnp.bfloat16)

def reference(frames_in, frame_time, norm_gain, w_query, w_key, w_value, w_output):
    count = frame_time.shape[0]
    normed = normed_rows(frames_in, norm_gain)
    query = jnp.dot(normed, w_query, preferred_element_type=jnp.float32).astype(jnp.bfloat16)
    keys = jnp.dot(normed, w_key, preferred_element_type=jnp.float32).astype(jnp.bfloat16)
    values = jnp.dot(normed, w_value, preferred_element_type=jnp.float32).astype(jnp.bfloat16)
    pooled_keys = lax.optimization_barrier(pooled(keys, count)).astype(jnp.float32)
    pooled_values = lax.optimization_barrier(pooled(values, count)).astype(jnp.float32)
    key_time = jnp.repeat(frame_time, PK)
    query_win = to_windows(query, count)
    keys_win = to_windows(keys, count)
    values_win = to_windows(values, count)
    factor = 1.0 / HD ** 0.5

    def one_frame(items):
        q_frame, k_frame, v_frame, t_frame = items
        q32 = q_frame.astype(jnp.float32)
        local_s = jnp.einsum('nqhd,nkhd->nhqk', q32, k_frame.astype(jnp.float32)) * factor
        far_s = jnp.einsum('nqhd,khd->nhqk', q32, pooled_keys) * factor
        valid = key_time < t_frame
        far_s = jnp.where(valid, far_s, -1e+30)
        top = jnp.maximum(lax.optimization_barrier(jnp.max(local_s, -1)), lax.optimization_barrier(jnp.max(far_s, -1)))
        local_w = jnp.exp(local_s - top[..., None])
        far_w = jnp.where(valid, jnp.exp(far_s - top[..., None]), 0.0)
        total = lax.optimization_barrier(jnp.sum(local_w, -1)) + lax.optimization_barrier(jnp.sum(far_w, -1))
        local_p = lax.optimization_barrier(local_w.astype(jnp.bfloat16)).astype(jnp.float32)
        far_p = lax.optimization_barrier(far_w.astype(jnp.bfloat16)).astype(jnp.float32)
        acc = jnp.einsum('nhqk,nkhd->nhqd', local_p, v_frame.astype(jnp.float32))
        acc = acc + jnp.einsum('nhqk,khd->nhqd', far_p, pooled_values)
        mixed = acc / total[..., None]
        return mixed.transpose(0, 2, 1, 3).astype(jnp.bfloat16)
    mixed = lax.map(one_frame, (query_win, keys_win, values_win, frame_time))
    mixed = from_windows(mixed, count)
    return jnp.dot(mixed, w_output, preferred_element_type=jnp.float32).astype(jnp.bfloat16)
```

```python
import functools

import jax
import jax.numpy as jnp
from jax import lax
from jax.experimental import pallas as pl
from jax.experimental.pallas import tpu as pltpu
from jax.sharding import PartitionSpec as P

HEADS = 6
HD = 128
HH = 16
WW = 16
WIN = 8
POOL = 4
TOKENS = HH * WW
PK = (HH // POOL) * (WW // POOL)
HALF = WIN * WW
NEG = -1e30
LOG2E = 1.4426950408889634
MESH = pl.DeviceIdType.MESH
NT = (((1,), (1,)), ((), ()))


def kernel(n, snake, ft, gain, x_hbm, wq_hbm, wk_hbm, wv_hbm, mixed,
           x_v, wq, wk, wv, normed, q_s, k_s, v_s, kg, vg, bias,
           x_sem, w_sem, ring_send, ring_recv, sib_send, sib_recv):
    rows = x_v.shape[0]
    count = rows // TOKENS
    own = count * PK
    keys = kg.shape[0]
    chips = n // 2
    me = lax.axis_index("tm")
    core = me % 2
    chip = me // 2
    half = chips // 2

    def chip_at(pos):
        pos = (pos + chips) % chips
        if not snake:
            return pos
        side = pos // half
        return (1 - side) * (2 * pos) + side * (2 * (chips - 1 - pos) + 1)

    if snake:
        place = (1 - chip % 2) * (chip // 2) + (chip % 2) * (chips - 1 - chip // 2)
    else:
        place = chip
    sibling = chip * 2 + (1 - core)
    step_of = (1, -1)
    neighbour = [chip_at(place + s) * 2 + core for s in step_of]
    reach = ((chips // 2, (chips - 1) // 2), ((chips - 1) // 2, chips // 2))

    blocks = x_sem.shape[0]
    size = rows // blocks
    loads = []
    for b in range(blocks):
        part = pl.ds(b * size, size)
        loads.append(pltpu.make_async_copy(x_hbm.at[part], x_v.at[part], x_sem.at[b]))
        loads[-1].start()
    weights = []
    for i, (src, dst) in enumerate(((wk_hbm, wk), (wv_hbm, wv), (wq_hbm, wq))):
        weights.append(pltpu.make_async_copy(src, dst, w_sem.at[i]))
        weights[-1].start()

    barrier = pltpu.get_barrier_semaphore()
    for other in (neighbour[0], neighbour[1], sibling):
        pl.semaphore_signal(barrier, inc=1, device_id={"tm": other}, device_id_type=MESH)

    slot = lax.broadcasted_iota(jnp.int32, (1, keys), 1) // PK

    def fill(s, kt):
        return jnp.where(slot == s, ft[s], kt)

    key_time = lax.fori_loop(0, ft.shape[0], fill, jnp.zeros((1, keys), jnp.int32))
    for f in range(count):
        bias[f] = jnp.where(key_time < ft[me * count + f], 0.0, NEG)

    sub = 32
    for b in range(blocks):
        loads[b].wait()

        def norm(i, carry, b=b):
            part = pl.ds(pl.multiple_of(b * size + i * sub, sub), sub)
            xf = x_v[part, :].astype(jnp.float32)
            scale = lax.rsqrt(jnp.mean(xf * xf, axis=-1, keepdims=True) + 1e-06)
            normed[part, :] = (xf * scale * gain[...]).astype(jnp.bfloat16)
            return carry

        lax.fori_loop(0, size // sub, norm, 0)

    tile = 256

    def project(w, out):
        def body(j, carry):
            cols = pl.ds(pl.multiple_of(j * tile, tile), tile)
            out[:, cols] = jnp.dot(
                normed[...], w[:, cols], preferred_element_type=jnp.float32
            ).astype(jnp.bfloat16)
            return carry

        lax.fori_loop(0, w.shape[1] // tile, body, 0)

    pr = lax.broadcasted_iota(jnp.int32, (own, rows), 0)
    pc = lax.broadcasted_iota(jnp.int32, (own, rows), 1)
    block_of = (pc // TOKENS) * PK + (pc % TOKENS) // (POOL * WW) * (WW // POOL) + (pc % WW) // POOL
    pool = jnp.where(pr == block_of, 1.0 / (POOL * POOL), 0.0).astype(jnp.bfloat16)

    gathered = (kg, vg)

    def rows_of(dev):
        return pl.ds(pl.multiple_of(dev * own, own), own)

    def origin(way, dist, plane):
        return chip_at(place - step_of[way] * dist) * 2 + plane

    def ring(way, dist, part):
        there = gathered[part].at[rows_of(origin(way, dist, core))]
        return pltpu.make_async_remote_copy(
            src_ref=there, dst_ref=there,
            send_sem=ring_send.at[way, dist, part], recv_sem=ring_recv.at[way, dist, part],
            device_id={"tm": neighbour[way]}, device_id_type=MESH)

    def arrived(way, dist, part):
        there = gathered[part].at[rows_of(origin(way, dist, core))]
        return pltpu.make_async_remote_copy(
            src_ref=there, dst_ref=there,
            send_sem=ring_send.at[way, dist - 1, part], recv_sem=ring_recv.at[way, dist - 1, part],
            device_id={"tm": neighbour[way]}, device_id_type=MESH)

    def across(way, dist, part, plane):
        there = gathered[part].at[rows_of(origin(way, dist, plane))]
        return pltpu.make_async_remote_copy(
            src_ref=there, dst_ref=there,
            send_sem=sib_send.at[way, dist, part], recv_sem=sib_recv.at[way, dist, part],
            device_id={"tm": sibling}, device_id_type=MESH)

    sends = []
    incoming = []

    def send_own(part):
        for way in (0, 1):
            if reach[way][part] > 0:
                copy = ring(way, 0, part)
                copy.start()
                sends.append(copy)
        copy = across(0, 0, part, core)
        copy.start()
        sends.append(copy)
        incoming.append(across(0, 0, part, 1 - core))

    def relay(dist, part):
        for way in (0, 1):
            if dist > reach[way][part]:
                continue
            arrived(way, dist, part).wait_recv()
            if dist < reach[way][part]:
                copy = ring(way, dist, part)
                copy.start()
                sends.append(copy)
            copy = across(way, dist, part, core)
            copy.start()
            sends.append(copy)
            incoming.append(across(way, dist, part, 1 - core))

    weights[0].wait()
    project(wk, k_s)
    kg[rows_of(me), :] = jnp.dot(pool, k_s[...], preferred_element_type=jnp.float32).astype(jnp.bfloat16)
    pl.semaphore_wait(barrier, 3)
    send_own(0)
    weights[1].wait()
    project(wv, v_s)
    vg[rows_of(me), :] = jnp.dot(pool, v_s[...], preferred_element_type=jnp.float32).astype(jnp.bfloat16)
    send_own(1)
    weights[2].wait()
    project(wq, q_s)
    for dist in range(1, chips // 2 + 1):
        for part in (0, 1):
            relay(dist, part)
    for copy in incoming:
        copy.wait_recv()

    ir = lax.broadcasted_iota(jnp.int32, (HALF, HALF), 0)
    ic = lax.broadcasted_iota(jnp.int32, (HALF, HALF), 1)
    near_bias = jnp.where((ir // WIN) % 2 == (ic // WIN) % 2, 0.0, NEG)
    rate = LOG2E / HD**0.5

    def attend(i, carry):
        f = i // (HEADS * 2)
        part = (i // HEADS) % 2
        h = i % HEADS
        cols = pl.ds(pl.multiple_of(h * HD, HD), HD)
        here = pl.ds(pl.multiple_of(f * TOKENS + part * HALF, HALF), HALF)
        q = q_s[here, cols]
        near = lax.dot_general(q, k_s[here, cols], NT, preferred_element_type=jnp.float32) + near_bias
        far = lax.dot_general(q, kg[:, cols], NT, preferred_element_type=jnp.float32) + bias[f]
        top = jnp.maximum(jnp.max(near, -1, keepdims=True), jnp.max(far, -1, keepdims=True))
        near_w = jnp.exp2((near - top) * rate)
        far_w = jnp.exp2((far - top) * rate)
        total = jnp.sum(near_w, -1, keepdims=True) + jnp.sum(far_w, -1, keepdims=True)
        acc = jnp.dot(near_w.astype(jnp.bfloat16), v_s[here, cols], preferred_element_type=jnp.float32)
        acc = acc + jnp.dot(far_w.astype(jnp.bfloat16), vg[:, cols], preferred_element_type=jnp.float32)
        mixed[here, cols] = (acc / total).astype(jnp.bfloat16)
        return carry

    lax.fori_loop(0, count * 2 * HEADS, attend, 0)
    for copy in sends:
        copy.wait_send()


def on_device(n, snake, frames_in, frame_time, norm_gain, w_query, w_key, w_value, w_output):
    rows, width = frames_in.shape
    inner = w_query.shape[1]
    count = rows // TOKENS
    keys = n * count * PK
    hops = n // 4 + 1
    bf = jnp.bfloat16
    dma = pltpu.SemaphoreType.DMA
    hbm = pl.BlockSpec(memory_space=pl.ANY)
    vmem = pl.BlockSpec(memory_space=pltpu.VMEM)
    mixed = pl.pallas_call(
        functools.partial(kernel, n, snake),
        out_shape=jax.ShapeDtypeStruct((rows, inner), bf),
        in_specs=[pl.BlockSpec(memory_space=pltpu.SMEM), vmem, hbm, hbm, hbm, hbm],
        out_specs=vmem,
        scratch_shapes=[
            pltpu.VMEM((rows, width), bf),
            pltpu.VMEM((width, inner), bf),
            pltpu.VMEM((width, inner), bf),
            pltpu.VMEM((width, inner), bf),
            pltpu.VMEM((rows, width), bf),
            pltpu.VMEM((rows, inner), bf),
            pltpu.VMEM((rows, inner), bf),
            pltpu.VMEM((rows, inner), bf),
            pltpu.VMEM((keys, inner), bf),
            pltpu.VMEM((keys, inner), bf),
            pltpu.VMEM((count, 1, keys), jnp.float32),
            dma((4,)),
            dma((3,)),
            dma((2, hops, 2)),
            dma((2, hops, 2)),
            dma((2, hops, 2)),
            dma((2, hops, 2)),
        ],
        compiler_params=pltpu.CompilerParams(
            collective_id=0, has_side_effects=True, vmem_limit_bytes=56 << 20
        ),
    )(frame_time, norm_gain.reshape(1, width), frames_in, w_query, w_key, w_value)
    return jnp.dot(mixed, w_output, preferred_element_type=jnp.float32).astype(bf)


def is_snake(mesh):
    names = list(mesh.axis_names)
    line = mesh.devices.transpose(names.index("grp"), names.index("tm"))[0]
    try:
        second = {d.coords[1] for d in line}
        third = {d.coords[2] for d in line}
    except (AttributeError, TypeError):
        return False
    return len(second) == 2 and len(third) * 4 == len(line)


def solution(mesh):
    placed = (P(("grp", "tm"), None), P("grp"), P(), P(), P(), P(), P())
    n = mesh.shape["tm"]
    return jax.shard_map(
        functools.partial(on_device, n, is_snake(mesh)),
        mesh=mesh, in_specs=placed, out_specs=P(("grp", "tm"), None), check_vma=False,
    )
```

```python
import functools

import jax
import jax.numpy as jnp
from jax import lax
from jax.experimental import pallas as pl
from jax.experimental.pallas import tpu as pltpu
from jax.sharding import PartitionSpec as P

HEADS = 6
HD = 128
HH = 16
WW = 16
WIN = 8
POOL = 4
TOKENS = HH * WW
PK = (HH // POOL) * (WW // POOL)
HALF = WIN * WW
NEG = -1e30
LOG2E = 1.4426950408889634
MESH = pl.DeviceIdType.MESH
NT = (((1,), (1,)), ((), ()))


def kernel(n, snake, near_reach, ft, gain, x_hbm, wq_hbm, wk_hbm, wv_hbm, mixed,
           x_v, wq, wk, wv, normed, q_s, k_s, v_s, far, bias, top_s, total_s, acc_s,
           x_sem, w_sem, ring_send, ring_recv, sib_send, sib_recv):
    rows = x_v.shape[0]
    count = rows // TOKENS
    own = count * PK
    pieces, keys, tile = far.shape
    parts = pieces // 2
    chips = n // 2
    me = lax.axis_index("tm")
    core = me % 2
    chip = me // 2
    half = chips // 2
    reach = (chips // 2, (chips - 1) // 2)

    def chip_at(pos):
        pos = (pos + chips) % chips
        if not snake:
            return pos
        side = pos // half
        return (1 - side) * (2 * pos) + side * (2 * (chips - 1 - pos) + 1)

    if snake:
        place = (1 - chip % 2) * (chip // 2) + (chip % 2) * (chips - 1 - chip // 2)
    else:
        place = chip
    sibling = chip * 2 + (1 - core)
    step_of = (1, -1)
    neighbour = [chip_at(place + s) * 2 + core for s in step_of]

    def limit(way, piece):
        return reach[way] if piece < parts else reach[1 - way]

    def place_of(way, dist, cross):
        if dist == 0:
            return cross * own
        first = (4 * dist - 2) * own
        if 2 * dist == chips:
            return first + cross * own
        return first + (2 * way + cross) * own

    blocks = x_sem.shape[0]
    size = rows // blocks
    loads = []
    for b in range(blocks):
        part = pl.ds(b * size, size)
        loads.append(pltpu.make_async_copy(x_hbm.at[part], x_v.at[part], x_sem.at[b]))
        loads[-1].start()
    weights = []
    for i, (src, dst) in enumerate(((wk_hbm, wk), (wv_hbm, wv), (wq_hbm, wq))):
        weights.append(pltpu.make_async_copy(src, dst, w_sem.at[i]))
        weights[-1].start()

    barrier = pltpu.get_barrier_semaphore()
    for other in (neighbour[0], neighbour[1], sibling):
        pl.semaphore_signal(barrier, inc=1, device_id={"tm": other}, device_id_type=MESH)

    sub = 32
    for b in range(blocks):
        loads[b].wait()

        def norm(i, carry, b=b):
            part = pl.ds(pl.multiple_of(b * size + i * sub, sub), sub)
            xf = x_v[part, :].astype(jnp.float32)
            scale = lax.rsqrt(jnp.mean(xf * xf, axis=-1, keepdims=True) + 1e-06)
            normed[part, :] = (xf * scale * gain[...]).astype(jnp.bfloat16)
            return carry

        lax.fori_loop(0, size // sub, norm, 0)

    pr = lax.broadcasted_iota(jnp.int32, (own, rows), 0)
    pc = lax.broadcasted_iota(jnp.int32, (own, rows), 1)
    block_of = (pc // TOKENS) * PK + (pc % TOKENS) // (POOL * WW) * (WW // POOL) + (pc % WW) // POOL
    pool = jnp.where(pr == block_of, 1.0 / (POOL * POOL), 0.0).astype(jnp.bfloat16)

    def ring(way, dist, piece):
        return pltpu.make_async_remote_copy(
            src_ref=far.at[piece, pl.ds(place_of(way, dist, 0), own)],
            dst_ref=far.at[piece, pl.ds(place_of(way, dist + 1, 0), own)],
            send_sem=ring_send.at[way, dist, piece], recv_sem=ring_recv.at[way, dist, piece],
            device_id={"tm": neighbour[way]}, device_id_type=MESH)

    def across(way, dist, piece):
        return pltpu.make_async_remote_copy(
            src_ref=far.at[piece, pl.ds(place_of(way, dist, 0), own)],
            dst_ref=far.at[piece, pl.ds(place_of(way, dist, 1), own)],
            send_sem=sib_send.at[way, dist, piece], recv_sem=sib_recv.at[way, dist, piece],
            device_id={"tm": sibling}, device_id_type=MESH)

    sends = []
    incoming = {}

    def send(way, dist, piece):
        if dist < limit(way, piece):
            copy = ring(way, dist, piece)
            copy.start()
            sends.append(copy)

    def share(way, dist, piece):
        copy = across(way, dist, piece)
        copy.start()
        sends.append(copy)
        incoming.setdefault(dist, []).append(copy)

    def relay(dist):
        for piece in range(pieces):
            for way in (0, 1):
                if dist <= limit(way, piece):
                    ring(way, dist - 1, piece).wait_recv()
                    send(way, dist, piece)
                    share(way, dist, piece)

    def settle(dists):
        for dist in dists:
            for copy in incoming[dist]:
                copy.wait_recv()

    def project(w, out, j):
        cols = pl.ds(j * tile, tile)
        out[:, cols] = jnp.dot(
            normed[...], w[:, cols], preferred_element_type=jnp.float32
        ).astype(jnp.bfloat16)

    for base, weight, w, out in ((0, weights[0], wk, k_s), (parts, weights[1], wv, v_s)):
        weight.wait()
        for j in range(parts):
            project(w, out, j)
            far[base + j, pl.ds(0, own), :] = jnp.dot(
                pool, out[:, pl.ds(j * tile, tile)], preferred_element_type=jnp.float32
            ).astype(jnp.bfloat16)
            if base + j == 0:
                pl.semaphore_wait(barrier, 3)
            for way in (0, 1):
                send(way, 0, base + j)
            share(0, 0, base + j)

    slot = lax.broadcasted_iota(jnp.int32, (1, keys), 1) // PK
    key_time = jnp.zeros((1, keys), jnp.int32)
    for dist in range(reach[0] + 1):
        for way in (0, 1):
            if (dist == 0 or 2 * dist == chips) and way == 1:
                continue
            for cross in (0, 1):
                plane = core * (1 - cross) + (1 - core) * cross
                dev = chip_at(place - step_of[way] * dist) * 2 + plane
                first = place_of(way, dist, cross) // PK
                for f in range(count):
                    key_time = jnp.where(slot == first + f, ft[dev * count + f], key_time)
    for f in range(count):
        bias[f] = jnp.where(key_time < ft[me * count + f], 0.0, NEG)

    weights[2].wait()
    for j in range(parts):
        project(wq, q_s, j)

    ir = lax.broadcasted_iota(jnp.int32, (HALF, HALF), 0)
    ic = lax.broadcasted_iota(jnp.int32, (HALF, HALF), 1)
    near_bias = jnp.where((ir // WIN) % 2 == (ic // WIN) % 2, 0.0, NEG)
    rate = LOG2E / HD**0.5
    cut = min(keys, (4 * near_reach + 2) * own)
    groups = tile // HD

    def first_pass(h, carry):
        cols = pl.ds(pl.multiple_of(h * HD, HD), HD)
        inner = pl.ds(pl.multiple_of(h % groups * HD, HD), HD)
        k_far = far[h // groups, pl.ds(0, cut), inner]
        v_far = far[parts + h // groups, pl.ds(0, cut), inner]
        for block in range(rows // HALF):
            here = pl.ds(block * HALF, HALF)
            q = q_s[here, cols]
            s0 = lax.dot_general(q, k_s[here, cols], NT, preferred_element_type=jnp.float32) + near_bias
            s1 = lax.dot_general(q, k_far, NT, preferred_element_type=jnp.float32)
            s1 = s1 + bias[block * HALF // TOKENS, :, pl.ds(0, cut)]
            top = jnp.maximum(jnp.max(s0, -1, keepdims=True), jnp.max(s1, -1, keepdims=True))
            w0 = jnp.exp2((s0 - top) * rate)
            w1 = jnp.exp2((s1 - top) * rate)
            total_s[h, here, :] = jnp.sum(w0, -1, keepdims=True) + jnp.sum(w1, -1, keepdims=True)
            top_s[h, here, :] = top
            acc = jnp.dot(w0.astype(jnp.bfloat16), v_s[here, cols], preferred_element_type=jnp.float32)
            acc_s[h, here, :] = acc + jnp.dot(w1.astype(jnp.bfloat16), v_far, preferred_element_type=jnp.float32)
        return carry

    def second_pass(h, carry):
        cols = pl.ds(pl.multiple_of(h * HD, HD), HD)
        inner = pl.ds(pl.multiple_of(h % groups * HD, HD), HD)
        k_far = far[h // groups, pl.ds(cut, keys - cut), inner]
        v_far = far[parts + h // groups, pl.ds(cut, keys - cut), inner]
        for block in range(rows // HALF):
            here = pl.ds(block * HALF, HALF)
            q = q_s[here, cols]
            s1 = lax.dot_general(q, k_far, NT, preferred_element_type=jnp.float32)
            s1 = s1 + bias[block * HALF // TOKENS, :, pl.ds(cut, keys - cut)]
            old = top_s[h, here, :]
            top = jnp.maximum(old, jnp.max(s1, -1, keepdims=True))
            keep = jnp.exp2((old - top) * rate)
            w1 = jnp.exp2((s1 - top) * rate)
            total = total_s[h, here, :] * keep + jnp.sum(w1, -1, keepdims=True)
            acc = jnp.dot(w1.astype(jnp.bfloat16), v_far, preferred_element_type=jnp.float32)
            acc = acc_s[h, here, :] * keep + acc
            mixed[here, cols] = (acc / total).astype(jnp.bfloat16)
        return carry

    for dist in range(1, near_reach + 1):
        relay(dist)
    settle(range(near_reach + 1))
    later = list(range(near_reach + 1, reach[0] + 1))
    spread = HEADS // 2
    lax.fori_loop(0, spread, first_pass, 0)
    for dist in later[:1]:
        relay(dist)
    lax.fori_loop(spread, HEADS, first_pass, 0)
    for dist in later[1:]:
        relay(dist)
    settle(later)
    lax.fori_loop(0, HEADS, second_pass, 0)
    for copy in sends:
        copy.wait_send()


def on_device(n, snake, frames_in, frame_time, norm_gain, w_query, w_key, w_value, w_output):
    rows, width = frames_in.shape
    inner = w_query.shape[1]
    count = rows // TOKENS
    keys = n * count * PK
    hops = n // 4 + 1
    tile = 2 * HD
    pieces = 2 * (inner // tile)
    near_reach = n // 8
    bf = jnp.bfloat16
    f32 = jnp.float32
    dma = pltpu.SemaphoreType.DMA
    hbm = pl.BlockSpec(memory_space=pl.ANY)
    vmem = pl.BlockSpec(memory_space=pltpu.VMEM)
    mixed = pl.pallas_call(
        functools.partial(kernel, n, snake, near_reach),
        out_shape=jax.ShapeDtypeStruct((rows, inner), bf),
        in_specs=[pl.BlockSpec(memory_space=pltpu.SMEM), vmem, hbm, hbm, hbm, hbm],
        out_specs=vmem,
        scratch_shapes=[
            pltpu.VMEM((rows, width), bf),
            pltpu.VMEM((width, inner), bf),
            pltpu.VMEM((width, inner), bf),
            pltpu.VMEM((width, inner), bf),
            pltpu.VMEM((rows, width), bf),
            pltpu.VMEM((rows, inner), bf),
            pltpu.VMEM((rows, inner), bf),
            pltpu.VMEM((rows, inner), bf),
            pltpu.VMEM((pieces, keys, tile), bf),
            pltpu.VMEM((count, 1, keys), f32),
            pltpu.VMEM((HEADS, rows, 1), f32),
            pltpu.VMEM((HEADS, rows, 1), f32),
            pltpu.VMEM((HEADS, rows, HD), f32),
            dma((4,)),
            dma((3,)),
            dma((2, hops, pieces)),
            dma((2, hops, pieces)),
            dma((2, hops, pieces)),
            dma((2, hops, pieces)),
        ],
        compiler_params=pltpu.CompilerParams(
            collective_id=0, has_side_effects=True, vmem_limit_bytes=56 << 20
        ),
    )(frame_time, norm_gain, frames_in, w_query, w_key, w_value)
    return jnp.dot(mixed, w_output, preferred_element_type=f32).astype(bf)


def is_snake(mesh):
    names = list(mesh.axis_names)
    line = mesh.devices.transpose(names.index("grp"), names.index("tm"))[0]
    try:
        second = {d.coords[1] for d in line}
        third = {d.coords[2] for d in line}
    except (AttributeError, TypeError):
        return False
    return len(second) == 2 and len(third) * 4 == len(line)


def solution(mesh):
    placed = (P(("grp", "tm"), None), P("grp"), P(), P(), P(), P(), P())
    n = mesh.shape["tm"]
    return jax.shard_map(
        functools.partial(on_device, n, is_snake(mesh)),
        mesh=mesh, in_specs=placed, out_specs=P(("grp", "tm"), None), check_vma=False,
    )
```

```python
import functools

import jax
import jax.numpy as jnp
from jax import lax
from jax.experimental import pallas as pl
from jax.experimental.pallas import tpu as pltpu
from jax.sharding import PartitionSpec as P

HEADS = 6
HD = 128
HH = 16
WW = 16
WIN = 8
POOL = 4
TOKENS = HH * WW
PK = (HH // POOL) * (WW // POOL)
HALF = WIN * WW
NEG = -1e30
LOG2E = 1.4426950408889634
MESH = pl.DeviceIdType.MESH
NT = (((1,), (1,)), ((), ()))


def kernel(n, snake, near_reach, ft, gain, x_hbm, wq_hbm, wk_hbm, wv_hbm, mixed,
           x_v, wq, wk, wv, normed, q_s, k_s, v_s, far, bias, top_s, acc_s, s_s, p_s,
           x_sem, w_sem, ring_send, ring_recv, sib_send, sib_recv):
    rows = x_v.shape[0]
    count = rows // TOKENS
    own = count * PK
    pieces, keys, tile = far.shape
    parts = pieces // 2
    chips = n // 2
    me = lax.axis_index("tm")
    core = me % 2
    chip = me // 2
    half = chips // 2
    reach = (chips // 2, (chips - 1) // 2)

    def chip_at(pos):
        pos = (pos + chips) % chips
        if not snake:
            return pos
        side = pos // half
        return (1 - side) * (2 * pos) + side * (2 * (chips - 1 - pos) + 1)

    if snake:
        place = (1 - chip % 2) * (chip // 2) + (chip % 2) * (chips - 1 - chip // 2)
    else:
        place = chip
    sibling = chip * 2 + (1 - core)
    step_of = (1, -1)
    neighbour = [chip_at(place + s) * 2 + core for s in step_of]

    def limit(way, piece):
        return reach[way] if piece < parts else reach[1 - way]

    def place_of(way, dist, cross):
        if dist == 0:
            return cross * own
        first = (4 * dist - 2) * own
        if 2 * dist == chips:
            return first + cross * own
        return first + (2 * way + cross) * own

    blocks = x_sem.shape[0]
    size = rows // blocks
    loads = []
    for b in range(blocks):
        part = pl.ds(b * size, size)
        loads.append(pltpu.make_async_copy(x_hbm.at[part], x_v.at[part], x_sem.at[b]))
        loads[-1].start()
    weights = []
    for i, (src, dst) in enumerate(((wk_hbm, wk), (wv_hbm, wv), (wq_hbm, wq))):
        weights.append(pltpu.make_async_copy(src, dst, w_sem.at[i]))
        weights[-1].start()

    barrier = pltpu.get_barrier_semaphore()
    for other in (neighbour[0], neighbour[1], sibling):
        pl.semaphore_signal(barrier, inc=1, device_id={"tm": other}, device_id_type=MESH)

    sub = 32
    for b in range(blocks):
        loads[b].wait()

        def norm(i, carry, b=b):
            part = pl.ds(pl.multiple_of(b * size + i * sub, sub), sub)
            xf = x_v[part, :].astype(jnp.float32)
            scale = lax.rsqrt(jnp.mean(xf * xf, axis=-1, keepdims=True) + 1e-06)
            normed[part, :] = (xf * scale * gain[...]).astype(jnp.bfloat16)
            return carry

        lax.fori_loop(0, size // sub, norm, 0)

    pr = lax.broadcasted_iota(jnp.int32, (own, rows), 0)
    pc = lax.broadcasted_iota(jnp.int32, (own, rows), 1)
    block_of = (pc // TOKENS) * PK + (pc % TOKENS) // (POOL * WW) * (WW // POOL) + (pc % WW) // POOL
    pool = jnp.where(pr == block_of, 1.0 / (POOL * POOL), 0.0).astype(jnp.bfloat16)

    def ring(way, dist, piece):
        return pltpu.make_async_remote_copy(
            src_ref=far.at[piece, pl.ds(place_of(way, dist, 0), own)],
            dst_ref=far.at[piece, pl.ds(place_of(way, dist + 1, 0), own)],
            send_sem=ring_send.at[way, dist, piece], recv_sem=ring_recv.at[way, dist, piece],
            device_id={"tm": neighbour[way]}, device_id_type=MESH)

    def across(way, dist, piece):
        return pltpu.make_async_remote_copy(
            src_ref=far.at[piece, pl.ds(place_of(way, dist, 0), own)],
            dst_ref=far.at[piece, pl.ds(place_of(way, dist, 1), own)],
            send_sem=sib_send.at[way, dist, piece], recv_sem=sib_recv.at[way, dist, piece],
            device_id={"tm": sibling}, device_id_type=MESH)

    sends = []
    incoming = {}

    def send(way, dist, piece):
        if dist < limit(way, piece):
            copy = ring(way, dist, piece)
            copy.start()
            sends.append(copy)

    def share(way, dist, piece):
        copy = across(way, dist, piece)
        copy.start()
        sends.append(copy)
        incoming.setdefault(dist, []).append(copy)

    def relay(dist):
        for piece in range(pieces):
            for way in (0, 1):
                if dist <= limit(way, piece):
                    ring(way, dist - 1, piece).wait_recv()
                    send(way, dist, piece)
                    share(way, dist, piece)

    def settle(dists):
        for dist in dists:
            for copy in incoming.get(dist, ()):
                copy.wait_recv()

    def project(w, out, j):
        cols = pl.ds(j * tile, tile)
        out[:, cols] = jnp.dot(
            normed[...], w[:, cols], preferred_element_type=jnp.float32
        ).astype(jnp.bfloat16)

    for base, weight, w, out in ((0, weights[0], wk, k_s), (parts, weights[1], wv, v_s)):
        weight.wait()
        for j in range(parts):
            project(w, out, j)
            far[base + j, pl.ds(0, own), :] = jnp.dot(
                pool, out[:, pl.ds(j * tile, tile)], preferred_element_type=jnp.float32
            ).astype(jnp.bfloat16)
            if base + j == 0:
                pl.semaphore_wait(barrier, 3)
            for way in (0, 1):
                send(way, 0, base + j)
            share(0, 0, base + j)

    slot = lax.broadcasted_iota(jnp.int32, (1, keys), 1) // PK
    key_time = jnp.zeros((1, keys), jnp.int32)
    for dist in range(reach[0] + 1):
        for way in (0, 1):
            if (dist == 0 or 2 * dist == chips) and way == 1:
                continue
            for cross in (0, 1):
                plane = core * (1 - cross) + (1 - core) * cross
                dev = chip_at(place - step_of[way] * dist) * 2 + plane
                first = place_of(way, dist, cross) // PK
                for f in range(count):
                    key_time = jnp.where(slot == first + f, ft[dev * count + f], key_time)
    for f in range(count):
        bias[f] = jnp.where(key_time < ft[me * count + f], 0.0, NEG)

    weights[2].wait()
    for j in range(parts):
        project(wq, q_s, j)

    ir = lax.broadcasted_iota(jnp.int32, (HALF, HALF), 0)
    ic = lax.broadcasted_iota(jnp.int32, (HALF, HALF), 1)
    near_bias = jnp.where((ir // WIN) % 2 == (ic // WIN) % 2, 0.0, NEG)
    rate = LOG2E / HD**0.5
    cut = min(keys, (4 * near_reach + 2) * own)
    groups = tile // HD

    ones = jnp.ones((1, HD), jnp.bfloat16)

    def with_ones(v):
        return jnp.concatenate([v, jnp.broadcast_to(ones, v.shape)], axis=1)

    def attend(h, lo, size, first, last):
        cols = pl.ds(pl.multiple_of(h * HD, HD), HD)
        inner = pl.ds(pl.multiple_of(h % groups * HD, HD), HD)
        span = pl.ds(0, size)
        k_far = far[h // groups, pl.ds(lo, size), inner]
        v_far = far[parts + h // groups, pl.ds(lo, size), inner]
        s_s[:, span] = lax.dot_general(q_s[:, cols], k_far, NT, preferred_element_type=jnp.float32)
        near = []
        keeps = []
        for block in range(rows // HALF):
            here = pl.ds(block * HALF, HALF)
            s = s_s[here, span] + bias[block * HALF // TOKENS, :, pl.ds(lo, size)]
            if first:
                s0 = lax.dot_general(q_s[here, cols], k_s[here, cols], NT, preferred_element_type=jnp.float32)
                s = jnp.concatenate([s0 + near_bias, s], axis=1)
            top = jnp.broadcast_to(jnp.max(s, -1, keepdims=True), (HALF, HD))
            if not first:
                old = top_s[h, here, :]
                top = jnp.maximum(old, top)
                keeps.append(jnp.exp2((old - top) * rate))
            if not last:
                top_s[h, here, :] = top
            w = jnp.exp2((s - jnp.tile(top, (1, -(-s.shape[1] // HD)))[:, :s.shape[1]]) * rate).astype(jnp.bfloat16)
            if first:
                near.append(jnp.dot(w[:, :HD], with_ones(v_s[here, cols]), preferred_element_type=jnp.float32))
                w = w[:, HD:]
            p_s[here, span] = w
        acc = jnp.dot(p_s[:, span], with_ones(v_far), preferred_element_type=jnp.float32)
        for block in range(rows // HALF):
            here = pl.ds(block * HALF, HALF)
            mine = acc[block * HALF:(block + 1) * HALF]
            if first:
                mine = mine + near[block]
            else:
                mine = mine + acc_s[h, here, :] * jnp.tile(keeps[block], (1, 2))
            if last:
                mixed[here, cols] = (mine[:, :HD] / mine[:, HD:]).astype(jnp.bfloat16)
            else:
                acc_s[h, here, :] = mine

    def first_pass(h, carry):
        attend(h, 0, cut, True, cut == keys)
        return carry

    def second_pass(h, carry):
        attend(h, cut, keys - cut, False, True)
        return carry

    for dist in range(1, near_reach + 1):
        relay(dist)
    settle(range(near_reach + 1))
    later = list(range(near_reach + 1, reach[0] + 1))
    spread = HEADS // 2
    lax.fori_loop(0, spread, first_pass, 0)
    for dist in later[:1]:
        relay(dist)
    lax.fori_loop(spread, HEADS, first_pass, 0)
    for dist in later[1:]:
        relay(dist)
    settle(later)
    if cut < keys:
        lax.fori_loop(0, HEADS, second_pass, 0)
    for copy in sends:
        copy.wait_send()


def on_device(n, snake, frames_in, frame_time, norm_gain, w_query, w_key, w_value, w_output):
    rows, width = frames_in.shape
    inner = w_query.shape[1]
    count = rows // TOKENS
    keys = n * count * PK
    hops = n // 4 + 1
    tile = 2 * HD
    pieces = 2 * (inner // tile)
    near_reach = n // 8
    bf = jnp.bfloat16
    f32 = jnp.float32
    dma = pltpu.SemaphoreType.DMA
    hbm = pl.BlockSpec(memory_space=pl.ANY)
    vmem = pl.BlockSpec(memory_space=pltpu.VMEM)
    mixed = pl.pallas_call(
        functools.partial(kernel, n, snake, near_reach),
        out_shape=jax.ShapeDtypeStruct((rows, inner), bf),
        in_specs=[pl.BlockSpec(memory_space=pltpu.SMEM), vmem, hbm, hbm, hbm, hbm],
        out_specs=vmem,
        scratch_shapes=[
            pltpu.VMEM((rows, width), bf),
            pltpu.VMEM((width, inner), bf),
            pltpu.VMEM((width, inner), bf),
            pltpu.VMEM((width, inner), bf),
            pltpu.VMEM((rows, width), bf),
            pltpu.VMEM((rows, inner), bf),
            pltpu.VMEM((rows, inner), bf),
            pltpu.VMEM((rows, inner), bf),
            pltpu.VMEM((pieces, keys, tile), bf),
            pltpu.VMEM((count, 1, keys), f32),
            pltpu.VMEM((HEADS, rows, HD), f32),
            pltpu.VMEM((HEADS, rows, 2 * HD), f32),
            pltpu.VMEM((rows, keys), f32),
            pltpu.VMEM((rows, keys), bf),
            dma((4,)),
            dma((3,)),
            dma((2, hops, pieces)),
            dma((2, hops, pieces)),
            dma((2, hops, pieces)),
            dma((2, hops, pieces)),
        ],
        compiler_params=pltpu.CompilerParams(
            collective_id=0, has_side_effects=True, vmem_limit_bytes=56 << 20
        ),
    )(frame_time, norm_gain, frames_in, w_query, w_key, w_value)
    return jnp.dot(mixed, w_output, preferred_element_type=f32).astype(bf)


def is_snake(mesh):
    names = list(mesh.axis_names)
    line = mesh.devices.transpose(names.index("grp"), names.index("tm"))[0]
    try:
        second = {d.coords[1] for d in line}
        third = {d.coords[2] for d in line}
    except (AttributeError, TypeError):
        return False
    return len(second) == 2 and len(third) * 4 == len(line)


def solution(mesh):
    placed = (P(("grp", "tm"), None), P("grp"), P(), P(), P(), P(), P())
    n = mesh.shape["tm"]
    return jax.shard_map(
        functools.partial(on_device, n, is_snake(mesh)),
        mesh=mesh, in_specs=placed, out_specs=P(("grp", "tm"), None), check_vma=False,
    )
```

```python
import functools

import jax
import jax.numpy as jnp
from jax import lax
from jax.experimental import pallas as pl
from jax.experimental.pallas import tpu as pltpu
from jax.sharding import PartitionSpec as P

HEADS = 6
HD = 128
HH = 16
WW = 16
WIN = 8
POOL = 4
TOKENS = HH * WW
PK = (HH // POOL) * (WW // POOL)
HALF = WIN * WW
NEG = -1e30
LOG2E = 1.4426950408889634
MESH = pl.DeviceIdType.MESH
NT = (((1,), (1,)), ((), ()))


def kernel(n, snake, near_reach, ft, gain, x_hbm, wq_hbm, wk_hbm, wv_hbm, mixed,
           x_v, wq, wk, wv, normed, q_s, k_s, v_s, far, bias, top_s, acc_s, s_s, p_s,
           x_sem, w_sem, ring_send, ring_recv, sib_send, sib_recv):
    rows = x_v.shape[0]
    count = rows // TOKENS
    own = count * PK
    pieces, keys, tile = far.shape
    parts = pieces // 2
    chips = n // 2
    me = lax.axis_index("tm")
    core = me % 2
    chip = me // 2
    half = chips // 2
    reach = (chips // 2, (chips - 1) // 2)

    def chip_at(pos):
        pos = (pos + chips) % chips
        if not snake:
            return pos
        side = pos // half
        return (1 - side) * (2 * pos) + side * (2 * (chips - 1 - pos) + 1)

    if snake:
        place = (1 - chip % 2) * (chip // 2) + (chip % 2) * (chips - 1 - chip // 2)
    else:
        place = chip
    sibling = chip * 2 + (1 - core)
    step_of = (1, -1)
    neighbour = [[chip_at(place + s * jump) * 2 + core for jump in (1, 2)] for s in step_of]

    def limit(way, piece):
        return reach[way] if piece < parts else reach[1 - way]

    def place_of(way, dist, cross):
        if dist == 0:
            return cross * own
        first = (4 * dist - 2) * own
        if 2 * dist == chips:
            return first + cross * own
        return first + (2 * way + cross) * own

    blocks = x_sem.shape[0]
    size = rows // blocks
    loads = []
    for b in range(blocks):
        part = pl.ds(b * size, size)
        loads.append(pltpu.make_async_copy(x_hbm.at[part], x_v.at[part], x_sem.at[b]))
        loads[-1].start()
    weights = []
    for i, (src, dst) in enumerate(((wk_hbm, wk), (wv_hbm, wv), (wq_hbm, wq))):
        weights.append(pltpu.make_async_copy(src, dst, w_sem.at[i]))
        weights[-1].start()

    barrier = pltpu.get_barrier_semaphore()
    for other in (*neighbour[0], *neighbour[1], sibling):
        pl.semaphore_signal(barrier, inc=1, device_id={"tm": other}, device_id_type=MESH)

    sub = 32
    for b in range(blocks):
        loads[b].wait()

        def norm(i, carry, b=b):
            part = pl.ds(pl.multiple_of(b * size + i * sub, sub), sub)
            xf = x_v[part, :].astype(jnp.float32)
            scale = lax.rsqrt(jnp.mean(xf * xf, axis=-1, keepdims=True) + 1e-06)
            normed[part, :] = (xf * scale * gain[...]).astype(jnp.bfloat16)
            return carry

        lax.fori_loop(0, size // sub, norm, 0)

    pr = lax.broadcasted_iota(jnp.int32, (own, rows), 0)
    pc = lax.broadcasted_iota(jnp.int32, (own, rows), 1)
    block_of = (pc // TOKENS) * PK + (pc % TOKENS) // (POOL * WW) * (WW // POOL) + (pc % WW) // POOL
    pool = jnp.where(pr == block_of, 1.0 / (POOL * POOL), 0.0).astype(jnp.bfloat16)

    def ring(way, dist, to, piece):
        return pltpu.make_async_remote_copy(
            src_ref=far.at[piece, pl.ds(place_of(way, dist, 0), own)],
            dst_ref=far.at[piece, pl.ds(place_of(way, to, 0), own)],
            send_sem=ring_send.at[way, to - 1, piece], recv_sem=ring_recv.at[way, to - 1, piece],
            device_id={"tm": neighbour[way][to - dist - 1]}, device_id_type=MESH)

    def across(way, dist, piece):
        return pltpu.make_async_remote_copy(
            src_ref=far.at[piece, pl.ds(place_of(way, dist, 0), own)],
            dst_ref=far.at[piece, pl.ds(place_of(way, dist, 1), own)],
            send_sem=sib_send.at[way, dist, piece], recv_sem=sib_recv.at[way, dist, piece],
            device_id={"tm": sibling}, device_id_type=MESH)

    sends = []
    incoming = {}

    def send(way, dist, piece):
        for to in (dist + 2, dist + 1):
            if dist % 2 == 0 and to <= limit(way, piece):
                copy = ring(way, dist, to, piece)
                copy.start()
                sends.append(copy)

    def share(way, dist, piece):
        copy = across(way, dist, piece)
        copy.start()
        sends.append(copy)
        incoming.setdefault(dist, []).append(copy)

    def relay(dist):
        for piece in range(pieces):
            for way in (0, 1):
                if dist <= limit(way, piece):
                    ring(way, (dist - 1) // 2 * 2, dist, piece).wait_recv()
                    send(way, dist, piece)
                    share(way, dist, piece)

    def settle(dists):
        for dist in dists:
            for copy in incoming.get(dist, ()):
                copy.wait_recv()

    def project(w, out, j):
        cols = pl.ds(j * tile, tile)
        out[:, cols] = jnp.dot(
            normed[...], w[:, cols], preferred_element_type=jnp.float32
        ).astype(jnp.bfloat16)

    for base, weight, w, out in ((0, weights[0], wk, k_s), (parts, weights[1], wv, v_s)):
        weight.wait()
        for j in range(parts):
            project(w, out, j)
            far[base + j, pl.ds(0, own), :] = jnp.dot(
                pool, out[:, pl.ds(j * tile, tile)], preferred_element_type=jnp.float32
            ).astype(jnp.bfloat16)
            if base + j == 0:
                pl.semaphore_wait(barrier, 5)
            for way in (0, 1):
                send(way, 0, base + j)
            share(0, 0, base + j)

    slot = lax.broadcasted_iota(jnp.int32, (1, keys), 1) // PK
    key_time = jnp.zeros((1, keys), jnp.int32)
    for dist in range(reach[0] + 1):
        for way in (0, 1):
            if (dist == 0 or 2 * dist == chips) and way == 1:
                continue
            for cross in (0, 1):
                plane = core * (1 - cross) + (1 - core) * cross
                dev = chip_at(place - step_of[way] * dist) * 2 + plane
                first = place_of(way, dist, cross) // PK
                for f in range(count):
                    key_time = jnp.where(slot == first + f, ft[dev * count + f], key_time)
    for f in range(count):
        bias[f] = jnp.where(key_time < ft[me * count + f], 0.0, NEG)

    weights[2].wait()
    for j in range(parts):
        project(wq, q_s, j)

    ir = lax.broadcasted_iota(jnp.int32, (HALF, HALF), 0)
    ic = lax.broadcasted_iota(jnp.int32, (HALF, HALF), 1)
    near_bias = jnp.where((ir // WIN) % 2 == (ic // WIN) % 2, 0.0, NEG)
    rate = LOG2E / HD**0.5
    cut = min(keys, (4 * near_reach + 2) * own)
    groups = tile // HD

    ones = jnp.ones((1, HD), jnp.bfloat16)

    def with_ones(v):
        return jnp.concatenate([v, jnp.broadcast_to(ones, v.shape)], axis=1)

    def attend(h, lo, size, first, last):
        cols = pl.ds(pl.multiple_of(h * HD, HD), HD)
        inner = pl.ds(pl.multiple_of(h % groups * HD, HD), HD)
        span = pl.ds(0, size)
        k_far = far[h // groups, pl.ds(lo, size), inner]
        v_far = far[parts + h // groups, pl.ds(lo, size), inner]
        s_s[:, span] = lax.dot_general(q_s[:, cols], k_far, NT, preferred_element_type=jnp.float32)
        near = []
        keeps = []
        for block in range(rows // HALF):
            here = pl.ds(block * HALF, HALF)
            s = s_s[here, span] + bias[block * HALF // TOKENS, :, pl.ds(lo, size)]
            if first:
                s0 = lax.dot_general(q_s[here, cols], k_s[here, cols], NT, preferred_element_type=jnp.float32)
                s = jnp.concatenate([s0 + near_bias, s], axis=1)
            top = jnp.broadcast_to(jnp.max(s, -1, keepdims=True), (HALF, HD))
            if not first:
                old = top_s[h, here, :]
                top = jnp.maximum(old, top)
                keeps.append(jnp.exp2((old - top) * rate))
            if not last:
                top_s[h, here, :] = top
            w = jnp.exp2((s - jnp.tile(top, (1, -(-s.shape[1] // HD)))[:, :s.shape[1]]) * rate).astype(jnp.bfloat16)
            if first:
                near.append(jnp.dot(w[:, :HD], with_ones(v_s[here, cols]), preferred_element_type=jnp.float32))
                w = w[:, HD:]
            p_s[here, span] = w
        acc = jnp.dot(p_s[:, span], with_ones(v_far), preferred_element_type=jnp.float32)
        for block in range(rows // HALF):
            here = pl.ds(block * HALF, HALF)
            mine = acc[block * HALF:(block + 1) * HALF]
            if first:
                mine = mine + near[block]
            else:
                mine = mine + acc_s[h, here, :] * jnp.tile(keeps[block], (1, 2))
            if last:
                mixed[here, cols] = (mine[:, :HD] / mine[:, HD:]).astype(jnp.bfloat16)
            else:
                acc_s[h, here, :] = mine

    def first_pass(h, carry):
        attend(h, 0, cut, True, cut == keys)
        return carry

    def second_pass(h, carry):
        attend(h, cut, keys - cut, False, True)
        return carry

    for dist in range(1, near_reach + 1):
        relay(dist)
    settle(range(near_reach + 1))
    later = list(range(near_reach + 1, reach[0] + 1))
    spread = HEADS // 2
    lax.fori_loop(0, spread, first_pass, 0)
    for dist in later[:1]:
        relay(dist)
    lax.fori_loop(spread, HEADS, first_pass, 0)
    for dist in later[1:]:
        relay(dist)
    settle(later)
    if cut < keys:
        lax.fori_loop(0, HEADS, second_pass, 0)
    for copy in sends:
        copy.wait_send()


def on_device(n, snake, frames_in, frame_time, norm_gain, w_query, w_key, w_value, w_output):
    rows, width = frames_in.shape
    inner = w_query.shape[1]
    count = rows // TOKENS
    keys = n * count * PK
    hops = n // 4 + 1
    tile = 2 * HD
    pieces = 2 * (inner // tile)
    near_reach = n // 8
    bf = jnp.bfloat16
    f32 = jnp.float32
    dma = pltpu.SemaphoreType.DMA
    hbm = pl.BlockSpec(memory_space=pl.ANY)
    vmem = pl.BlockSpec(memory_space=pltpu.VMEM)
    mixed = pl.pallas_call(
        functools.partial(kernel, n, snake, near_reach),
        out_shape=jax.ShapeDtypeStruct((rows, inner), bf),
        in_specs=[pl.BlockSpec(memory_space=pltpu.SMEM), vmem, hbm, hbm, hbm, hbm],
        out_specs=vmem,
        scratch_shapes=[
            pltpu.VMEM((rows, width), bf),
            pltpu.VMEM((width, inner), bf),
            pltpu.VMEM((width, inner), bf),
            pltpu.VMEM((width, inner), bf),
            pltpu.VMEM((rows, width), bf),
            pltpu.VMEM((rows, inner), bf),
            pltpu.VMEM((rows, inner), bf),
            pltpu.VMEM((rows, inner), bf),
            pltpu.VMEM((pieces, keys, tile), bf),
            pltpu.VMEM((count, 1, keys), f32),
            pltpu.VMEM((HEADS, rows, HD), f32),
            pltpu.VMEM((HEADS, rows, 2 * HD), f32),
            pltpu.VMEM((rows, keys), f32),
            pltpu.VMEM((rows, keys), bf),
            dma((4,)),
            dma((3,)),
            dma((2, hops, pieces)),
            dma((2, hops, pieces)),
            dma((2, hops, pieces)),
            dma((2, hops, pieces)),
        ],
        compiler_params=pltpu.CompilerParams(
            collective_id=0, has_side_effects=True, vmem_limit_bytes=56 << 20
        ),
    )(frame_time, norm_gain, frames_in, w_query, w_key, w_value)
    return jnp.dot(mixed, w_output, preferred_element_type=f32).astype(bf)


def is_snake(mesh):
    names = list(mesh.axis_names)
    line = mesh.devices.transpose(names.index("grp"), names.index("tm"))[0]
    try:
        second = {d.coords[1] for d in line}
        third = {d.coords[2] for d in line}
    except (AttributeError, TypeError):
        return False
    return len(second) == 2 and len(third) * 4 == len(line)


def solution(mesh):
    placed = (P(("grp", "tm"), None), P("grp"), P(), P(), P(), P(), P())
    n = mesh.shape["tm"]
    return jax.shard_map(
        functools.partial(on_device, n, is_snake(mesh)),
        mesh=mesh, in_specs=placed, out_specs=P(("grp", "tm"), None), check_vma=False,
    )
```
